32 devices in a mesh: groups: 2 (over y), expert: 8 (over z, core), sub: 2 (over x).
Axes of the slice: x: 2, y: 2, z: 4, core: 2. Of those that a mesh axis runs over, the one named last changes fastest.
Arguments:
- latent: bfloat16 [4096, 1024], P(('groups', 'expert', 'sub')), parts along dimension 0, may hold values from -6 to 6
- routes: int32 [4096, 4], P(('groups', 'expert', 'sub')), parts along dimension 0, may hold values from 0 to 7, all different within a row; in each aligned block of 128 rows (0 to 127, 128 to 255, ...) at most 96 rows name the same one
- gates: float32 [4096, 4], P(('groups', 'expert', 'sub')), parts along dimension 0, may hold values from 0.1 to 1
- up_weight: bfloat16 [8, 1024, 2688], P('expert', None, 'sub'), may hold values from -0.1875 to 0.1875
- down_weight: bfloat16 [8, 1024, 2688], P('expert', None, 'sub'), may hold values from -0.125 to 0.125
Outputs:
- mixed: bfloat16 [4096, 1024], P(('groups', 'expert', 'sub')), parts along dimension 0
The draws below stay inside these ranges and needn't reach their ends.
There are 2 independent parts, one for each index of `groups`. The reference program is written for one: setup_inputs(seed, part) draws one part's arguments, and reference() takes and returns one part's arrays. A program takes and returns all parts, laid end to end along the dimension named above; an argument that names none is the same for every part. Nothing has to cross between parts.
Inputs may be any that keep to these rules, and one draw needn't show every extreme that they name: `routes`: each token names 4 different experts; among the 128 tokens of one device no expert is named more than 96 times, a bound that some block reaches.
All inputs are finite; a program needn't handle non-finite values.
Results may differ from the reference program's by a relative error of at most 0.0058.
Values may be sent and summed in bfloat16 or wider, within the bound.
A program may use at most 128 MiB of HBM per device.

```python
import math
import jax
import jax.numpy as jnp
import numpy as np
from jax import lax

LATENT = 1024
HIDDEN_SIZE = 2688
TOK_DEV = 128
TOPK = 4
EXPERTS = 8
MOST = 96
TOKENS = 2048


def levels(key, shape, split, least, high):
    loudness = 1.0
    for axis_at, parts in split:
        steps = jax.random.uniform(jax.random.fold_in(jax.random.fold_in(key, 6), axis_at), (parts,), jnp.float32, least / len(split), high / len(split))
        loudness = loudness * jnp.repeat(jnp.exp(steps), shape[axis_at] // parts).reshape((-1,) + (1,) * (len(shape) - 1 - axis_at))
    return loudness


def shared_out(stream_key, own, number, rows, number_of, top, limit, slope):
    order = jax.random.permutation(stream_key, number_of)
    heavy_load, ordinary = load_shares(number_of, rows * top, limit, slope, True), load_shares(number_of, rows * top, limit, slope, False)
    places = jnp.arange(number_of)

    def named(tallies, offset_by):
        used = int((tallies > 0).sum())
        fixed = max(1, used // 4)
        shifted = fixed + (places - fixed + offset_by * (used - fixed)) % max(1, number_of - fixed)
        return jnp.zeros((number_of,), jnp.int32).at[order[jnp.where(places < fixed, places, shifted)]].set(jnp.asarray(tallies, jnp.int32))

    tallies = jnp.where(number % 4 == 0, named(heavy_load, number // 4), named(ordinary, number - number // 4 - 1))
    mixed = jax.random.permutation(jax.random.fold_in(own, 3), number_of)
    donor, receiver = mixed[0:number_of // 2 * 2:2], mixed[1:number_of // 2 * 2:2]
    margin = jnp.minimum(tallies[donor] - 1, limit - tallies[receiver]) // 2
    margin = jnp.where((donor == order[0]) | (receiver == order[0]) | (tallies[receiver] == 0), 0, jnp.maximum(margin, 0))
    shifted = jax.random.randint(jax.random.fold_in(own, 4), (number_of // 2,), 0, 1 << 20) % (margin + 1)
    tallies = tallies.at[donor].add(-shifted).at[receiver].add(shifted)
    members = jnp.searchsorted(jnp.cumsum(tallies), jnp.arange(rows * top), side="right").astype(jnp.int32)
    listing = members.reshape(top, rows).T
    listing = listing[jax.random.permutation(jax.random.fold_in(own, 1), rows)]
    offset_by = jax.random.randint(jax.random.fold_in(own, 2), (rows, 1), 0, top)
    return jnp.take_along_axis(listing, (jnp.arange(top)[None, :] + offset_by) % top, axis=1)


def load_shares(amount, total, limit, lean, full):
    weights = [(1 << 20) // math.isqrt(grade ** lean) + 1 for grade in range(1, amount + 1)]
    largest = limit if full else min(limit, max(-(-total // amount), total * weights[0] // sum(weights)))
    least = 1 if total - largest >= amount - 1 else 0
    given, rest = [largest] + [least] * (amount - 1), total - largest - least * (amount - 1)
    while rest > 0:
        movable = [i for i in range(1, amount) if given[i] < largest] or [i for i in range(1, amount) if given[i] < limit]
        pool, left = sum([weights[i] for i in movable]), rest
        for i in movable:
            more = min(limit - given[i], max(1, left * weights[i] // pool), rest)
            given[i] = given[i] + more
            rest = rest - more
    return np.array(given)


def centred(key, extent, spread, reach, split=(), kind=jnp.bfloat16):
    array = spread * jax.random.normal(key, extent, jnp.float32)
    if split:
        array = array * levels(key, extent, split, -0.22, 0.18)
    return jnp.clip(array, -reach, reach).astype(kind)


def setup_inputs(seed: int = 0, part: int = 0) -> dict:
    key_of = jax.random.split(jax.random.key(seed), 6)
    part_keys = jax.random.split(jax.random.fold_in(key_of[5], part), 6)
    latent = centred(part_keys[0], (TOKENS, LATENT), 1.0, 6.0, ((0, 16),))
    routes_keys = jax.random.split(jax.random.fold_in(part_keys[1], 1), TOKENS // TOK_DEV)
    routes_turns = jax.random.permutation(jax.random.fold_in(part_keys[1], 3), TOKENS // TOK_DEV)
    routes = jax.vmap(lambda own, number: shared_out(jax.random.fold_in(part_keys[1], 2), own, number, TOK_DEV, EXPERTS, TOPK, MOST, 2))(routes_keys, routes_turns).reshape((TOKENS, TOPK))
    gates = jnp.clip(0.1 + 0.9 * jax.random.uniform(part_keys[2], (TOKENS, TOPK), jnp.float32) ** levels(part_keys[2], (TOKENS, TOPK), ((0, 16),), -0.2, 0.2), 0.1, 1.0)
    up_weight = centred(key_of[3], (EXPERTS, LATENT, HIDDEN_SIZE), LATENT ** -0.5, 0.1875, ((0, 8), (2, 2)))
    down_weight = centred(key_of[4], (EXPERTS, LATENT, HIDDEN_SIZE), HIDDEN_SIZE ** -0.5, 0.125, ((0, 8), (2, 2)))
    return dict(latent=latent, routes=routes, gates=gates, up_weight=up_weight, down_weight=down_weight)


def expert_rows(gathered, up_part, down_part):
    preact = jnp.dot(gathered, up_part, preferred_element_type=jnp.float32)
    active = jnp.square(jnp.maximum(preact, 0.0)).astype(jnp.bfloat16)
    return lax.dot_general(active, down_part, (((1,), (1,)), ((), ())), preferred_element_type=jnp.float32)


def reference(latent, routes, gates, up_weight, down_weight):
    pair_count = TOKENS * TOPK
    route_ids = routes.reshape(-1).astype(jnp.int32)
    tok_index = jnp.arange(pair_count, dtype=jnp.int32) // TOPK
    flat_gate = gates.reshape(-1)
    padded = jnp.concatenate([latent, jnp.zeros((1, LATENT), latent.dtype)], axis=0)
    capacity = (TOKENS // TOK_DEV) * MOST

    def one_expert(carry, expert):
        chosen = jnp.nonzero(route_ids == expert, size=capacity, fill_value=pair_count)[0].astype(jnp.int32)
        is_live = chosen < pair_count
        clipped = jnp.minimum(chosen, pair_count - 1).astype(jnp.int32)
        token_of = jnp.where(is_live, tok_index[clipped], TOKENS).astype(jnp.int32)
        gathered = padded[token_of]
        rounded = expert_rows(gathered, up_weight[expert], down_weight[expert]).astype(jnp.bfloat16)
        rounded = lax.optimization_barrier(rounded).astype(jnp.float32)
        weight = jnp.where(is_live, flat_gate[clipped], jnp.float32(0.0))
        carry = carry.at[token_of].add(weight[:, None] * rounded)
        return carry, None

    summed = lax.scan(one_expert, jnp.zeros((TOKENS + 1, LATENT), jnp.float32), jnp.arange(EXPERTS, dtype=jnp.int32))[0]
    return summed[:TOKENS].astype(jnp.bfloat16)
```

```python
import jax
import jax.numpy as jnp
from jax import lax
from jax.sharding import PartitionSpec as P

TEAM = ("expert", "sub")


def local(latent, routes, gates, up_weight, down_weight):
    experts = lax.axis_size("expert")
    chosen = routes[:, :, None] == jnp.arange(experts, dtype=jnp.int32)[None, None, :]
    share = jnp.sum(jnp.where(chosen, gates[:, :, None], 0.0), axis=1)
    rows = lax.all_gather(latent, TEAM, axis=0, tiled=True)
    shares = lax.all_gather(share, TEAM, axis=0, tiled=True)
    mine = lax.axis_index("expert")
    weight = jnp.sum(
        jnp.where(jnp.arange(experts)[None, :] == mine, shares, 0.0), axis=1, keepdims=True
    )
    preact = jnp.dot(rows, up_weight[0], preferred_element_type=jnp.float32)
    active = jnp.square(jnp.maximum(preact, 0.0)).astype(jnp.bfloat16)
    part = lax.dot_general(
        active, down_weight[0], (((1,), (1,)), ((), ())), preferred_element_type=jnp.float32
    )
    part = (part * weight).astype(jnp.bfloat16)
    return lax.psum_scatter(part, TEAM, scatter_dimension=0, tiled=True)


def solution(mesh):
    placed = (
        P(("groups", "expert", "sub"), None),
        P(("groups", "expert", "sub"), None),
        P(("groups", "expert", "sub"), None),
        P("expert", None, "sub"),
        P("expert", None, "sub"),
    )
    return jax.shard_map(
        local,
        mesh=mesh,
        in_specs=placed,
        out_specs=P(("groups", "expert", "sub"), None),
        check_vma=False,
    )
```

```python
import functools

import jax
import jax.numpy as jnp
from jax import lax
from jax.experimental import pallas as pl
from jax.experimental.pallas import tpu as pltpu
from jax.sharding import PartitionSpec as P

CORES = 2
VMEM_MOST = 60 * 1024 * 1024
F32, BF16 = jnp.float32, jnp.bfloat16


def expert_part(row_block, up_part, down_part):
    preact = jnp.dot(row_block, up_part, preferred_element_type=F32)
    active = jnp.square(jnp.maximum(preact, 0.0)).astype(BF16)
    return lax.dot_general(
        active, down_part, (((1,), (1,)), ((), ())), preferred_element_type=F32
    )


def routed(latent, routes, gates, up_weight, down_weight):
    tokens_here, row_width = latent.shape
    top_count = routes.shape[1]
    experts = lax.axis_size("expert")
    slot_most = min(tokens_here, 3 * tokens_here * top_count // (2 * experts))
    pair_count = tokens_here * top_count
    route_ids = routes.reshape(-1)
    one_hot = (route_ids[:, None] == jnp.arange(experts, dtype=jnp.int32)[None, :]).astype(
        jnp.int32
    )
    before = jnp.cumsum(one_hot, axis=0) - one_hot
    slot_rank = jnp.sum(before * one_hot, axis=1)
    slot_of = route_ids * slot_most + slot_rank
    source = (
        jnp.full((experts * slot_most,), pair_count, jnp.int32)
        .at[slot_of]
        .set(jnp.arange(pair_count, dtype=jnp.int32))
    )
    padded = jnp.concatenate([latent, jnp.zeros((1, row_width), latent.dtype)], axis=0)
    send_rows = padded[source // top_count].reshape(experts, slot_most, row_width)
    arrived = lax.all_to_all(send_rows, "expert", split_axis=0, concat_axis=0, tiled=True)
    flat_rows = arrived.reshape(-1, row_width)
    summed = expert_part(
        flat_rows,
        lax.all_gather(up_weight, "sub", axis=2, tiled=True)[0],
        lax.all_gather(down_weight, "sub", axis=2, tiled=True)[0],
    )
    expert_out = lax.all_to_all(
        summed.astype(BF16).reshape(arrived.shape),
        "expert",
        split_axis=0,
        concat_axis=0,
        tiled=True,
    )
    values = expert_out.reshape(experts * slot_most, row_width)[slot_of].astype(F32)
    mixed_out = jnp.sum(
        values.reshape(tokens_here, top_count, row_width) * gates[:, :, None], axis=1
    )
    return mixed_out.astype(BF16)


def team_kernel(
    lanes,
    latent_ref, share_ref, up_hbm, down_hbm, out_ref,
    rows, shares, up, down, kept, sib_out, sib_in, x_out, x_in, lane_out, lane_in,
    w_sem, lane_s, lane_r, x_s, x_r, sib_s, sib_r,
    rsib_s, rsib_r, rx_s, rx_r, rlane_s, rlane_r,
):
    tokens = latent_ref.shape[0]
    me = lax.axis_index("expert")
    sub = lax.axis_index("sub")
    chip, core = me // CORES, me % CORES
    sibling = {"expert": chip * CORES + 1 - core}
    partner = {"sub": 1 - sub}
    bits = lanes.bit_length() - 1

    def lane_peer(step):
        place = 0
        for bit in range(bits):
            size = 1 << bit
            place = place + size * ((chip // size + step // size) % 2)
        return {"expert": place * CORES + core}

    def send(src, dst, s_sem, r_sem, device):
        return pltpu.make_async_remote_copy(
            src_ref=src, dst_ref=dst, send_sem=s_sem, recv_sem=r_sem,
            device_id=device, device_id_type=pl.DeviceIdType.MESH,
        )

    own = (latent_ref, share_ref)
    boxes = (rows, shares)

    def to_lane(kind, step):
        return send(own[kind], boxes[kind].at[0, step, 0], lane_s.at[kind, step],
                    lane_r.at[kind, step], lane_peer(step))

    def to_sub(kind, step, src=None):
        src = boxes[kind].at[0, step, 0] if src is None else src
        return send(src, boxes[kind].at[1, step, 0], x_s.at[kind, step],
                    x_r.at[kind, step], partner)

    def to_sibling(kind, other, step, src=None):
        src = boxes[kind].at[other, step, 0] if src is None else src
        return send(src, boxes[kind].at[other, step, 1], sib_s.at[kind, other, step],
                    sib_r.at[kind, other, step], sibling)

    def back_sibling(other, step):
        return send(sib_out.at[other, step], sib_in.at[other, step], rsib_s.at[other, step],
                    rsib_r.at[other, step], sibling)

    def back_sub(step):
        return send(x_out.at[step], x_in.at[step], rx_s.at[step], rx_r.at[step], partner)

    def back_lane(step):
        return send(lane_out.at[step], lane_in.at[step], rlane_s.at[step],
                    rlane_r.at[step], lane_peer(step))

    up_copy = pltpu.make_async_copy(up_hbm.at[0], up, w_sem.at[0])
    down_copy = pltpu.make_async_copy(down_hbm.at[0], down, w_sem.at[1])
    up_copy.start()
    down_copy.start()

    barrier = pltpu.get_barrier_semaphore()
    greeted = [sibling, partner] + [lane_peer(step) for step in range(1, lanes)]
    for device in greeted:
        pl.semaphore_signal(barrier, inc=1, device_id=device,
                            device_id_type=pl.DeviceIdType.MESH)
    pl.semaphore_wait(barrier, len(greeted))

    for kind in (1, 0):
        to_sub(kind, 0, own[kind]).start()
        to_sibling(kind, 0, 0, own[kind]).start()
        for step in range(1, lanes):
            to_lane(kind, step).start()
    rows[0, 0, 0] = latent_ref[...]
    shares[0, 0, 0] = share_ref[...]
    up_copy.wait()
    down_copy.wait()

    def finish_sub(step):
        back_sibling(1, step).wait_recv()
        total = kept[1, step] + sib_in[1, step].astype(F32)
        x_out[step] = total.astype(BF16)
        back_sub(step).start()

    def gate_column(other, step, side):
        line = shares[other, step, side, me]
        spot = lax.broadcasted_iota(jnp.int32, (tokens, tokens), 0) == lax.broadcasted_iota(
            jnp.int32, (tokens, tokens), 1
        )
        return jnp.sum(jnp.where(spot, line, 0.0), axis=1, keepdims=True)

    def one(index, carry):
        step, other = index // 2, index % 2

        @pl.when((other == 1) & (step + 1 < lanes))
        def _():
            for kind in (0, 1):
                to_lane(kind, step + 1).wait_recv()
                to_sub(kind, step + 1).start()
                to_sibling(kind, 0, step + 1).start()

        @pl.when(other == 1)
        def _():
            for kind in (0, 1):
                to_sub(kind, step).wait_recv()
                to_sibling(kind, 1, step).start()

        for kind in (0, 1):
            to_sibling(kind, other, step).wait_recv()
        block = rows[other, step].reshape(2 * tokens, rows.shape[-1])
        part = expert_part(block, up[...], down[...])
        kept[other, step] = part[:tokens] * gate_column(other, step, 0)
        sib_out[other, step] = (part[tokens:] * gate_column(other, step, 1)).astype(BF16)
        back_sibling(other, step).start()

        @pl.when((other == 0) & (step >= 2))
        def _():
            finish_sub(step - 1)

        return carry

    lax.fori_loop(0, 2 * lanes, one, 0)

    if lanes > 1:
        finish_sub(lanes - 1)
    finish_sub(0)

    def column_total(step):
        back_sibling(0, step).wait_recv()
        back_sub(step).wait_recv()
        return kept[0, step] + sib_in[0, step].astype(F32) + x_in[step].astype(F32)

    for step in range(1, lanes):
        lane_out[step] = column_total(step).astype(BF16)
        back_lane(step).start()
    total = column_total(0)
    for step in range(1, lanes):
        back_lane(step).wait_recv()
        total = total + lane_in[step].astype(F32)
    out_ref[...] = total.astype(BF16)

    for step in range(lanes):
        for kind in (0, 1):
            to_sub(kind, step).wait_send()
            for other in (0, 1):
                to_sibling(kind, other, step).wait_send()
            if step:
                to_lane(kind, step).wait_send()
        for other in (0, 1):
            back_sibling(other, step).wait_send()
        back_sub(step).wait_send()
        if step:
            back_lane(step).wait_send()


def team(latent, routes, gates, up_weight, down_weight):
    tokens, width = latent.shape
    hidden = up_weight.shape[2]
    experts = lax.axis_size("expert")
    lanes = experts // CORES
    chosen = routes[None, :, :] == jnp.arange(experts, dtype=jnp.int32)[:, None, None]
    share = jnp.sum(jnp.where(chosen, gates[None, :, :], 0.0), axis=2).reshape(experts, 1, tokens)
    vmem = pl.BlockSpec(memory_space=pltpu.VMEM)
    hbm = pl.BlockSpec(memory_space=pl.ANY)
    dma = pltpu.SemaphoreType.DMA
    return pl.pallas_call(
        functools.partial(team_kernel, lanes),
        out_shape=jax.ShapeDtypeStruct((tokens, width), BF16),
        in_specs=[vmem, vmem, hbm, hbm],
        out_specs=vmem,
        scratch_shapes=[
            pltpu.VMEM((2, lanes, 2, tokens, width), BF16),
            pltpu.VMEM((2, lanes, 2, experts, 1, tokens), F32),
            pltpu.VMEM((width, hidden), BF16),
            pltpu.VMEM((width, hidden), BF16),
            pltpu.VMEM((2, lanes, tokens, width), F32),
            pltpu.VMEM((2, lanes, tokens, width), BF16),
            pltpu.VMEM((2, lanes, tokens, width), BF16),
            pltpu.VMEM((lanes, tokens, width), BF16),
            pltpu.VMEM((lanes, tokens, width), BF16),
            pltpu.VMEM((lanes, tokens, width), BF16),
            pltpu.VMEM((lanes, tokens, width), BF16),
            dma((2,)),
            dma((2, lanes)), dma((2, lanes)), dma((2, lanes)), dma((2, lanes)),
            dma((2, 2, lanes)), dma((2, 2, lanes)),
            dma((2, lanes)), dma((2, lanes)),
            dma((lanes,)), dma((lanes,)), dma((lanes,)), dma((lanes,)),
        ],
        compiler_params=pltpu.CompilerParams(
            collective_id=0, has_side_effects=True, vmem_limit_bytes=VMEM_MOST
        ),
    )(latent, share, up_weight, down_weight)


def local(latent, routes, gates, up_weight, down_weight):
    tokens, width = latent.shape
    experts, subs = lax.axis_size("expert"), lax.axis_size("sub")
    lanes = experts // CORES
    block = tokens * width * 2
    need = block * lanes * (4 + 4 + 2 + 2 + 4) + 4 * up_weight.size + 16 * block
    fits = subs == 2 and lanes & (lanes - 1) == 0 and need < VMEM_MOST
    plan = team if fits and experts % CORES == 0 and tokens % 128 == 0 else routed
    return plan(latent, routes, gates, up_weight, down_weight)


def solution(mesh):
    placed = (
        P(("groups", "expert", "sub"), None),
        P(("groups", "expert", "sub"), None),
        P(("groups", "expert", "sub"), None),
        P("expert", None, "sub"),
        P("expert", None, "sub"),
    )
    return jax.shard_map(
        local,
        mesh=mesh,
        in_specs=placed,
        out_specs=P(("groups", "expert", "sub"), None),
        check_vma=False,
    )
```

```python
import functools

import jax
import jax.numpy as jnp
from jax import lax
from jax.experimental import pallas as pl
from jax.experimental.pallas import tpu as pltpu
from jax.sharding import PartitionSpec as P

CORES = 2
VMEM_MOST = 60 * 1024 * 1024
F32, BF16 = jnp.float32, jnp.bfloat16


def expert_part(row_block, up_part, down_part):
    preact = jnp.dot(row_block, up_part, preferred_element_type=F32)
    active = jnp.square(jnp.maximum(preact, 0.0)).astype(BF16)
    return lax.dot_general(
        active, down_part, (((1,), (1,)), ((), ())), preferred_element_type=F32
    )


def routed(latent, routes, gates, up_weight, down_weight):
    tokens_here, row_width = latent.shape
    top_count = routes.shape[1]
    experts = lax.axis_size("expert")
    slot_most = min(tokens_here, 3 * tokens_here * top_count // (2 * experts))
    pair_count = tokens_here * top_count
    route_ids = routes.reshape(-1)
    one_hot = (route_ids[:, None] == jnp.arange(experts, dtype=jnp.int32)[None, :]).astype(
        jnp.int32
    )
    before = jnp.cumsum(one_hot, axis=0) - one_hot
    slot_rank = jnp.sum(before * one_hot, axis=1)
    slot_of = route_ids * slot_most + slot_rank
    source = (
        jnp.full((experts * slot_most,), pair_count, jnp.int32)
        .at[slot_of]
        .set(jnp.arange(pair_count, dtype=jnp.int32))
    )
    padded = jnp.concatenate([latent, jnp.zeros((1, row_width), latent.dtype)], axis=0)
    send_rows = padded[source // top_count].reshape(experts, slot_most, row_width)
    arrived = lax.all_to_all(send_rows, "expert", split_axis=0, concat_axis=0, tiled=True)
    flat_rows = arrived.reshape(-1, row_width)
    summed = expert_part(
        flat_rows,
        lax.all_gather(up_weight, "sub", axis=2, tiled=True)[0],
        lax.all_gather(down_weight, "sub", axis=2, tiled=True)[0],
    )
    expert_out = lax.all_to_all(
        summed.astype(BF16).reshape(arrived.shape),
        "expert",
        split_axis=0,
        concat_axis=0,
        tiled=True,
    )
    values = expert_out.reshape(experts * slot_most, row_width)[slot_of].astype(F32)
    mixed_out = jnp.sum(
        values.reshape(tokens_here, top_count, row_width) * gates[:, :, None], axis=1
    )
    return mixed_out.astype(BF16)


def team_kernel(
    lanes,
    latent_ref, share_ref, up_hbm, down_hbm, out_ref,
    rows, shares, up, down, kept, sib_out, sib_in, x_out, x_in, lane_out, lane_in,
    w_sem, lane_s, lane_r, x_s, x_r, sib_s, sib_r,
    rsib_s, rsib_r, rx_s, rx_r, rlane_s, rlane_r,
):
    tokens = latent_ref.shape[0]
    me = lax.axis_index("expert")
    sub = lax.axis_index("sub")
    chip, core = me // CORES, me % CORES
    sibling = {"expert": chip * CORES + 1 - core}
    partner = {"sub": 1 - sub}
    bits = lanes.bit_length() - 1

    def lane_peer(step):
        place = 0
        for bit in range(bits):
            size = 1 << bit
            place = place + size * ((chip // size + step // size) % 2)
        return {"expert": place * CORES + core}

    def send(src, dst, s_sem, r_sem, device):
        return pltpu.make_async_remote_copy(
            src_ref=src, dst_ref=dst, send_sem=s_sem, recv_sem=r_sem,
            device_id=device, device_id_type=pl.DeviceIdType.MESH,
        )

    own = (latent_ref, share_ref)
    boxes = (rows, shares)

    def to_lane(kind, step, hops=None, src=None, slot=None):
        hops = step if hops is None else hops
        src = own[kind] if src is None else boxes[kind].at[0, src, 0]
        slot = step if slot is None else slot
        return send(src, boxes[kind].at[0, step, 0], lane_s.at[kind, slot],
                    lane_r.at[kind, step], lane_peer(hops))

    relay = lanes == 4
    inner = ((chip + 1) // 2) % 2 == 1

    def relayed(kind, what):
        if what == 0:
            return to_lane(kind, 2, 3, 1, 2)
        if what == 1:
            return to_lane(kind, 2, 1, 3, 4)
        return to_lane(kind, 3, 1, 2, 5)

    def to_sub(kind, step, src=None):
        src = boxes[kind].at[0, step, 0] if src is None else src
        return send(src, boxes[kind].at[1, step, 0], x_s.at[kind, step],
                    x_r.at[kind, step], partner)

    def to_sibling(kind, other, step, src=None):
        src = boxes[kind].at[other, step, 0] if src is None else src
        return send(src, boxes[kind].at[other, step, 1], sib_s.at[kind, other, step],
                    sib_r.at[kind, other, step], sibling)

    def back_sibling(other, step):
        return send(sib_out.at[other, step], sib_in.at[other, step], rsib_s.at[other, step],
                    rsib_r.at[other, step], sibling)

    def back_sub(step):
        return send(x_out.at[step], x_in.at[step], rx_s.at[step], rx_r.at[step], partner)

    def back_lane(step):
        return send(lane_out.at[step], lane_in.at[step], rlane_s.at[step],
                    rlane_r.at[step], lane_peer(step))

    up_copy = pltpu.make_async_copy(up_hbm.at[0], up, w_sem.at[0])
    down_copy = pltpu.make_async_copy(down_hbm.at[0], down, w_sem.at[1])
    up_copy.start()
    down_copy.start()

    barrier = pltpu.get_barrier_semaphore()
    greeted = [sibling, partner] + [lane_peer(step) for step in range(1, lanes)]
    for device in greeted:
        pl.semaphore_signal(barrier, inc=1, device_id=device,
                            device_id_type=pl.DeviceIdType.MESH)
    pl.semaphore_wait(barrier, len(greeted))

    for kind in (1, 0):
        to_sub(kind, 0, own[kind]).start()
        to_sibling(kind, 0, 0, own[kind]).start()
        if relay:
            to_lane(kind, 1).start()

            @pl.when(inner)
            def _():
                to_lane(kind, 3).start()
        else:
            for step in range(1, lanes):
                to_lane(kind, step).start()
    rows[0, 0, 0] = latent_ref[...]
    shares[0, 0, 0] = share_ref[...]
    up_copy.wait()
    down_copy.wait()

    def finish_sub(step):
        back_sibling(1, step).wait_recv()
        total = kept[1, step] + sib_in[1, step].astype(F32)
        x_out[step] = total.astype(BF16)
        back_sub(step).start()

    def gate_column(other, step, side):
        line = shares[other, step, side, me]
        spot = lax.broadcasted_iota(jnp.int32, (tokens, tokens), 0) == lax.broadcasted_iota(
            jnp.int32, (tokens, tokens), 1
        )
        return jnp.sum(jnp.where(spot, line, 0.0), axis=1, keepdims=True)

    def one(index, carry):
        step, other = index // 2, index % 2

        @pl.when((other == 1) & (step + 1 < lanes))
        def _():
            if relay:
                @pl.when(jnp.logical_not(inner & (step == 2)))
                def _():
                    for kind in (0, 1):
                        to_lane(kind, step + 1).wait_recv()

                @pl.when(inner & (step == 0))
                def _():
                    for kind in (0, 1):
                        relayed(kind, 0).start()
                    for kind in (0, 1):
                        to_lane(kind, 3).wait_recv()
                        relayed(kind, 1).start()

                @pl.when(inner & (step == 1))
                def _():
                    for kind in (0, 1):
                        relayed(kind, 2).start()
            else:
                for kind in (0, 1):
                    to_lane(kind, step + 1).wait_recv()
            for kind in (0, 1):
                to_sub(kind, step + 1).start()
                to_sibling(kind, 0, step + 1).start()

        @pl.when(other == 1)
        def _():
            for kind in (0, 1):
                to_sub(kind, step).wait_recv()
                to_sibling(kind, 1, step).start()

        for kind in (0, 1):
            to_sibling(kind, other, step).wait_recv()
        block = rows[other, step].reshape(2 * tokens, rows.shape[-1])
        preact = lax.dot_general(
            block, up[...], (((1,), (1,)), ((), ())), preferred_element_type=F32
        )
        active = jnp.square(jnp.maximum(preact, 0.0)).astype(BF16)
        part = jnp.dot(active, down[...], preferred_element_type=F32)
        kept[other, step] = part[:tokens] * gate_column(other, step, 0)
        sib_out[other, step] = (part[tokens:] * gate_column(other, step, 1)).astype(BF16)
        back_sibling(other, step).start()

        @pl.when((other == 0) & (step >= 3))
        def _():
            finish_sub(step - 1)

        return carry

    lax.fori_loop(0, 2 * lanes, one, 0)

    for step in (*range(min(lanes, 3) - 1, 0, -1), 0) if lanes < 4 else (lanes - 1, 1, 0):
        finish_sub(step)

    def column_total(step):
        back_sibling(0, step).wait_recv()
        back_sub(step).wait_recv()
        return kept[0, step] + sib_in[0, step].astype(F32) + x_in[step].astype(F32)

    for step in (*range(2, lanes), 1) if lanes > 1 else ():
        lane_out[step] = column_total(step).astype(BF16)
        back_lane(step).start()
    total = column_total(0)
    for step in range(1, lanes):
        back_lane(step).wait_recv()
        total = total + lane_in[step].astype(F32)
    out_ref[...] = total.astype(BF16)

    for step in range(lanes):
        for kind in (0, 1):
            to_sub(kind, step).wait_send()
            for other in (0, 1):
                to_sibling(kind, other, step).wait_send()
            if step == 1 or (step and not relay):
                to_lane(kind, step).wait_send()
        for other in (0, 1):
            back_sibling(other, step).wait_send()
        back_sub(step).wait_send()
        if step:
            back_lane(step).wait_send()
    if relay:
        @pl.when(inner)
        def _():
            for kind in (0, 1):
                to_lane(kind, 3).wait_send()
                for what in range(3):
                    relayed(kind, what).wait_send()


def team(latent, routes, gates, up_weight, down_weight):
    tokens, width = latent.shape
    hidden = up_weight.shape[2]
    experts = lax.axis_size("expert")
    lanes = experts // CORES
    chosen = routes[None, :, :] == jnp.arange(experts, dtype=jnp.int32)[:, None, None]
    share = jnp.sum(jnp.where(chosen, gates[None, :, :], 0.0), axis=2).reshape(experts, 1, tokens)
    vmem = pl.BlockSpec(memory_space=pltpu.VMEM)
    hbm = pl.BlockSpec(memory_space=pl.ANY)
    dma = pltpu.SemaphoreType.DMA
    return pl.pallas_call(
        functools.partial(team_kernel, lanes),
        out_shape=jax.ShapeDtypeStruct((tokens, width), BF16),
        in_specs=[vmem, vmem, hbm, hbm],
        out_specs=vmem,
        scratch_shapes=[
            pltpu.VMEM((2, lanes, 2, tokens, width), BF16),
            pltpu.VMEM((2, lanes, 2, experts, 1, tokens), F32),
            pltpu.VMEM((hidden, width), BF16),
            pltpu.VMEM((hidden, width), BF16),
            pltpu.VMEM((2, lanes, tokens, width), F32),
            pltpu.VMEM((2, lanes, tokens, width), BF16),
            pltpu.VMEM((2, lanes, tokens, width), BF16),
            pltpu.VMEM((lanes, tokens, width), BF16),
            pltpu.VMEM((lanes, tokens, width), BF16),
            pltpu.VMEM((lanes, tokens, width), BF16),
            pltpu.VMEM((lanes, tokens, width), BF16),
            dma((2,)),
            dma((2, lanes + 2)), dma((2, lanes)), dma((2, lanes)), dma((2, lanes)),
            dma((2, 2, lanes)), dma((2, 2, lanes)),
            dma((2, lanes)), dma((2, lanes)),
            dma((lanes,)), dma((lanes,)), dma((lanes,)), dma((lanes,)),
        ],
        compiler_params=pltpu.CompilerParams(
            collective_id=0, has_side_effects=True, vmem_limit_bytes=VMEM_MOST
        ),
    )(latent, share, jnp.swapaxes(up_weight, 1, 2), jnp.swapaxes(down_weight, 1, 2))


def local(latent, routes, gates, up_weight, down_weight):
    tokens, width = latent.shape
    experts, subs = lax.axis_size("expert"), lax.axis_size("sub")
    lanes = experts // CORES
    block = tokens * width * 2
    need = block * lanes * (4 + 4 + 2 + 2 + 4) + 4 * up_weight.size + 16 * block
    fits = subs == 2 and lanes & (lanes - 1) == 0 and need < VMEM_MOST
    plan = team if fits and experts % CORES == 0 and tokens % 128 == 0 else routed
    return plan(latent, routes, gates, up_weight, down_weight)


def solution(mesh):
    placed = (
        P(("groups", "expert", "sub"), None),
        P(("groups", "expert", "sub"), None),
        P(("groups", "expert", "sub"), None),
        P("expert", None, "sub"),
        P("expert", None, "sub"),
    )
    return jax.shard_map(
        local,
        mesh=mesh,
        in_specs=placed,
        out_specs=P(("groups", "expert", "sub"), None),
        check_vma=False,
    )
```

```python
import functools

import jax
import jax.numpy as jnp
from jax import lax
from jax.experimental import pallas as pl
from jax.experimental.pallas import tpu as pltpu
from jax.sharding import PartitionSpec as P

CORES = 2
PIECES = 2
VMEM_MOST = 60 * 1024 * 1024
F32, BF16 = jnp.float32, jnp.bfloat16


def expert_part(row_block, up_part, down_part):
    preact = jnp.dot(row_block, up_part, preferred_element_type=F32)
    active = jnp.square(jnp.maximum(preact, 0.0)).astype(BF16)
    return lax.dot_general(
        active, down_part, (((1,), (1,)), ((), ())), preferred_element_type=F32
    )


def routed(latent, routes, gates, up_weight, down_weight):
    tokens_here, row_width = latent.shape
    top_count = routes.shape[1]
    experts = lax.axis_size("expert")
    slot_most = min(tokens_here, 3 * tokens_here * top_count // (2 * experts))
    pair_count = tokens_here * top_count
    route_ids = routes.reshape(-1)
    one_hot = (route_ids[:, None] == jnp.arange(experts, dtype=jnp.int32)[None, :]).astype(
        jnp.int32
    )
    before = jnp.cumsum(one_hot, axis=0) - one_hot
    slot_rank = jnp.sum(before * one_hot, axis=1)
    slot_of = route_ids * slot_most + slot_rank
    source = (
        jnp.full((experts * slot_most,), pair_count, jnp.int32)
        .at[slot_of]
        .set(jnp.arange(pair_count, dtype=jnp.int32))
    )
    padded = jnp.concatenate([latent, jnp.zeros((1, row_width), latent.dtype)], axis=0)
    send_rows = padded[source // top_count].reshape(experts, slot_most, row_width)
    arrived = lax.all_to_all(send_rows, "expert", split_axis=0, concat_axis=0, tiled=True)
    flat_rows = arrived.reshape(-1, row_width)
    summed = expert_part(
        flat_rows,
        lax.all_gather(up_weight, "sub", axis=2, tiled=True)[0],
        lax.all_gather(down_weight, "sub", axis=2, tiled=True)[0],
    )
    expert_out = lax.all_to_all(
        summed.astype(BF16).reshape(arrived.shape),
        "expert",
        split_axis=0,
        concat_axis=0,
        tiled=True,
    )
    values = expert_out.reshape(experts * slot_most, row_width)[slot_of].astype(F32)
    mixed_out = jnp.sum(
        values.reshape(tokens_here, top_count, row_width) * gates[:, :, None], axis=1
    )
    return mixed_out.astype(BF16)


def team_kernel(
    lanes,
    latent_ref, share_ref, up_hbm, down_hbm, out_ref,
    rows, shares, up, down, kept, sib_out, sib_in, x_out, x_in, lane_out, lane_in,
    w_sem, lane_s, lane_r, x_s, x_r, sib_s, sib_r,
    rsib_s, rsib_r, rx_s, rx_r, rlane_s, rlane_r, next_s, mid_r, lane_mid, lane_sum,
):
    tokens = latent_ref.shape[0]
    me = lax.axis_index("expert")
    sub = lax.axis_index("sub")
    chip, core = me // CORES, me % CORES
    sibling = {"expert": chip * CORES + 1 - core}
    partner = {"sub": 1 - sub}
    bits = lanes.bit_length() - 1

    def lane_peer(step):
        place = 0
        for bit in range(bits):
            size = 1 << bit
            place = place + size * ((chip // size + step // size) % 2)
        return {"expert": place * CORES + core}

    def send(src, dst, s_sem, r_sem, device):
        return pltpu.make_async_remote_copy(
            src_ref=src, dst_ref=dst, send_sem=s_sem, recv_sem=r_sem,
            device_id=device, device_id_type=pl.DeviceIdType.MESH,
        )

    own = (latent_ref, share_ref)
    boxes = (rows, shares)

    def to_lane(kind, step, hops=None, src=None, slot=None):
        hops = step if hops is None else hops
        src = own[kind] if src is None else boxes[kind].at[0, src, 0]
        slot = step if slot is None else slot
        return send(src, boxes[kind].at[0, step, 0], lane_s.at[kind, slot],
                    lane_r.at[kind, step], lane_peer(hops))

    relay = lanes == 4
    inner = ((chip + 1) // 2) % 2 == 1

    def relayed(kind, what):
        if what == 0:
            return to_lane(kind, 2, 3, 1, 2)
        if what == 1:
            return to_lane(kind, 2, 1, 3, 4)
        return to_lane(kind, 3, 1, 2, 5)

    def to_sub(kind, step, src=None):
        src = boxes[kind].at[0, step, 0] if src is None else src
        return send(src, boxes[kind].at[1, step, 0], x_s.at[kind, step],
                    x_r.at[kind, step], partner)

    around = 2 * jnp.where(inner, 1, 0)

    def crossing(step):
        return jnp.where(inner & (step == 1), 3, step)

    def to_next(kind):
        return send(boxes[kind].at[1, around, 0], boxes[kind].at[1, around + 1, 0],
                    next_s.at[kind], x_r.at[kind, around + 1], lane_peer(1))

    def to_sibling(kind, other, step, src=None):
        src = boxes[kind].at[other, step, 0] if src is None else src
        return send(src, boxes[kind].at[other, step, 1], sib_s.at[kind, other, step],
                    sib_r.at[kind, other, step], sibling)

    def back_sibling(other, step):
        return send(sib_out.at[other, step], sib_in.at[other, step], rsib_s.at[other, step],
                    rsib_r.at[other, step], sibling)

    def back_sub(step, piece):
        return send(x_out.at[step, piece], x_in.at[step, piece], rx_s.at[step, piece],
                    rx_r.at[step, piece], partner)

    def back_lane(step, piece, src=None):
        src = lane_out if src is None else src
        return send(src.at[step, piece], lane_in.at[step, piece],
                    rlane_s.at[step, piece], rlane_r.at[step, piece], lane_peer(step))

    def to_inner(step, piece):
        return send(lane_out.at[step, piece], lane_mid.at[5 - step, piece],
                    rlane_s.at[step, piece], mid_r.at[5 - step, piece], lane_peer(1))

    def span(piece):
        return pl.ds(piece * (tokens // PIECES), tokens // PIECES)

    up_copy = pltpu.make_async_copy(up_hbm.at[0], up, w_sem.at[0])
    down_copy = pltpu.make_async_copy(down_hbm.at[0], down, w_sem.at[1])
    up_copy.start()
    down_copy.start()

    barrier = pltpu.get_barrier_semaphore()
    greeted = [sibling, partner] + [lane_peer(step) for step in range(1, lanes)]
    for device in greeted:
        pl.semaphore_signal(barrier, inc=1, device_id=device,
                            device_id_type=pl.DeviceIdType.MESH)
    pl.semaphore_wait(barrier, len(greeted))

    for kind in (1, 0):
        to_sub(kind, 0, own[kind]).start()
        to_sibling(kind, 0, 0, own[kind]).start()
        if relay:
            to_lane(kind, 1).start()

            @pl.when(inner)
            def _():
                to_lane(kind, 3).start()
        else:
            for step in range(1, lanes):
                to_lane(kind, step).start()
    rows[0, 0, 0] = latent_ref[...]
    shares[0, 0, 0] = share_ref[...]
    up_copy.wait()
    down_copy.wait()

    def finish_sub(step):
        back_sibling(1, step).wait_recv()
        for piece in range(PIECES):
            total = kept[1, step, span(piece)] + sib_in[1, step, span(piece)].astype(F32)
            x_out[step, piece] = total.astype(BF16)
            back_sub(step, piece).start()

    def gate_column(other, step, side):
        line = shares[other, step, side, me]
        spot = lax.broadcasted_iota(jnp.int32, (tokens, tokens), 0) == lax.broadcasted_iota(
            jnp.int32, (tokens, tokens), 1
        )
        return jnp.sum(jnp.where(spot, line, 0.0), axis=1, keepdims=True)

    def one(index, carry):
        step, other = index // 2, index % 2

        @pl.when((other == 1) & (step + 1 < lanes))
        def _():
            if relay:
                @pl.when(jnp.logical_not(inner & (step == 2)))
                def _():
                    for kind in (0, 1):
                        to_lane(kind, step + 1).wait_recv()

                @pl.when(inner & (step == 0))
                def _():
                    for kind in (0, 1):
                        relayed(kind, 0).start()
                    for kind in (0, 1):
                        to_lane(kind, 3).wait_recv()
                        relayed(kind, 1).start()

                @pl.when(inner & (step == 1))
                def _():
                    for kind in (0, 1):
                        relayed(kind, 2).start()
            else:
                for kind in (0, 1):
                    to_lane(kind, step + 1).wait_recv()
            for kind in (0, 1):
                if relay:
                    @pl.when(step < 2)
                    def _():
                        to_sub(kind, crossing(step + 1)).start()
                else:
                    to_sub(kind, step + 1).start()
                to_sibling(kind, 0, step + 1).start()

        @pl.when(other == 1)
        def _():
            for kind in (0, 1):
                to_sub(kind, step).wait_recv()
                if relay:
                    @pl.when(step == around)
                    def _():
                        to_next(kind).start()
                to_sibling(kind, 1, step).start()

        for kind in (0, 1):
            to_sibling(kind, other, step).wait_recv()
        block = rows[other, step].reshape(2 * tokens, rows.shape[-1])
        preact = lax.dot_general(
            block, up[...], (((1,), (1,)), ((), ())), preferred_element_type=F32
        )
        active = jnp.square(jnp.maximum(preact, 0.0)).astype(BF16)
        part = jnp.dot(active, down[...], preferred_element_type=F32)
        kept[other, step] = part[:tokens] * gate_column(other, step, 0)
        sib_out[other, step] = (part[tokens:] * gate_column(other, step, 1)).astype(BF16)
        back_sibling(other, step).start()

        @pl.when((other == 0) & (step >= 3))
        def _():
            finish_sub(step - 1)

        return carry

    lax.fori_loop(0, 2 * lanes, one, 0)

    for step in (*range(min(lanes, 3) - 1, 0, -1), 0) if lanes < 4 else (lanes - 1, 1, 0):
        finish_sub(step)

    def column_total(step, piece):
        back_sub(step, piece).wait_recv()
        total = kept[0, step, span(piece)] + sib_in[0, step, span(piece)].astype(F32)
        return total + x_in[step, piece].astype(F32)

    for step in range(lanes):
        back_sibling(0, step).wait_recv()
    def returned(step, piece):
        if not relay or step == 1:
            back_lane(step, piece).start()
            return

        @pl.when(inner)
        def _():
            to_inner(5 - step, piece).wait_recv()
            total = lane_out[step, piece].astype(F32) + lane_mid[step, piece].astype(F32)
            lane_sum[step, piece] = total.astype(BF16)
            back_lane(step, piece, lane_sum).start()

        @pl.when(jnp.logical_not(inner))
        def _():
            to_inner(step, piece).start()

    for step in (*range(2, lanes), 1) if lanes > 1 else ():
        for piece in range(PIECES):
            lane_out[step, piece] = column_total(step, piece).astype(BF16)
            returned(step, piece)
    near = 2 + jnp.where(inner, 1, 0)
    for piece in range(PIECES):
        total = column_total(0, piece)
        for step in (1, near) if relay else range(1, lanes):
            back_lane(step, piece).wait_recv()
            total = total + lane_in[step, piece].astype(F32)
        out_ref[span(piece), :] = total.astype(BF16)

    for step in range(lanes):
        for kind in (0, 1):
            if not relay:
                to_sub(kind, step).wait_send()
            elif step < 3:
                to_sub(kind, crossing(step)).wait_send()
            else:
                to_next(kind).wait_send()
            for other in (0, 1):
                to_sibling(kind, other, step).wait_send()
            if step == 1 or (step and not relay):
                to_lane(kind, step).wait_send()
        for other in (0, 1):
            back_sibling(other, step).wait_send()
        for piece in range(PIECES):
            back_sub(step, piece).wait_send()
            if step:
                back_lane(step, piece).wait_send()
    if relay:
        @pl.when(inner)
        def _():
            for kind in (0, 1):
                to_lane(kind, 3).wait_send()
                for what in range(3):
                    relayed(kind, what).wait_send()


def team(latent, routes, gates, up_weight, down_weight):
    tokens, width = latent.shape
    hidden = up_weight.shape[2]
    experts = lax.axis_size("expert")
    lanes = experts // CORES
    chosen = routes[None, :, :] == jnp.arange(experts, dtype=jnp.int32)[:, None, None]
    share = jnp.sum(jnp.where(chosen, gates[None, :, :], 0.0), axis=2).reshape(experts, 1, tokens)
    vmem = pl.BlockSpec(memory_space=pltpu.VMEM)
    hbm = pl.BlockSpec(memory_space=pl.ANY)
    dma = pltpu.SemaphoreType.DMA
    return pl.pallas_call(
        functools.partial(team_kernel, lanes),
        out_shape=jax.ShapeDtypeStruct((tokens, width), BF16),
        in_specs=[vmem, vmem, hbm, hbm],
        out_specs=vmem,
        scratch_shapes=[
            pltpu.VMEM((2, lanes, 2, tokens, width), BF16),
            pltpu.VMEM((2, lanes, 2, experts, 1, tokens), F32),
            pltpu.VMEM((hidden, width), BF16),
            pltpu.VMEM((hidden, width), BF16),
            pltpu.VMEM((2, lanes, tokens, width), F32),
            pltpu.VMEM((2, lanes, tokens, width), BF16),
            pltpu.VMEM((2, lanes, tokens, width), BF16),
            pltpu.VMEM((lanes, PIECES, tokens // PIECES, width), BF16),
            pltpu.VMEM((lanes, PIECES, tokens // PIECES, width), BF16),
            pltpu.VMEM((lanes, PIECES, tokens // PIECES, width), BF16),
            pltpu.VMEM((lanes, PIECES, tokens // PIECES, width), BF16),
            dma((2,)),
            dma((2, lanes + 2)), dma((2, lanes)), dma((2, lanes)), dma((2, lanes)),
            dma((2, 2, lanes)), dma((2, 2, lanes)),
            dma((2, lanes)), dma((2, lanes)),
            dma((lanes, PIECES)), dma((lanes, PIECES)), dma((lanes, PIECES)), dma((lanes, PIECES)),
            dma((2,)),
            dma((lanes, PIECES)),
            pltpu.VMEM((lanes, PIECES, tokens // PIECES, width), BF16),
            pltpu.VMEM((lanes, PIECES, tokens // PIECES, width), BF16),
        ],
        compiler_params=pltpu.CompilerParams(
            collective_id=0, has_side_effects=True, vmem_limit_bytes=VMEM_MOST
        ),
    )(latent, share, jnp.swapaxes(up_weight, 1, 2), jnp.swapaxes(down_weight, 1, 2))


def local(latent, routes, gates, up_weight, down_weight):
    tokens, width = latent.shape
    experts, subs = lax.axis_size("expert"), lax.axis_size("sub")
    lanes = experts // CORES
    block = tokens * width * 2
    need = block * lanes * (4 + 4 + 2 + 2 + 4) + 4 * up_weight.size + 16 * block
    fits = subs == 2 and lanes & (lanes - 1) == 0 and need < VMEM_MOST
    plan = team if fits and experts % CORES == 0 and tokens % 128 == 0 else routed
    return plan(latent, routes, gates, up_weight, down_weight)


def solution(mesh):
    placed = (
        P(("groups", "expert", "sub"), None),
        P(("groups", "expert", "sub"), None),
        P(("groups", "expert", "sub"), None),
        P("expert", None, "sub"),
        P("expert", None, "sub"),
    )
    return jax.shard_map(
        local,
        mesh=mesh,
        in_specs=placed,
        out_specs=P(("groups", "expert", "sub"), None),
        check_vma=False,
    )
```
